128 devices in a mesh: section: 8 (over y, core), seq: 16 (over z, x).
Axes of the slice: x: 4, y: 4, z: 4, core: 2. Of those that a mesh axis runs over, the one named last changes fastest.
Arguments:
- queries: bfloat16 [8, 2, 2048, 4096], P('section', None, 'seq'), may hold values from -20 to 20
- keys_values: bfloat16 [8, 2, 2048, 8, 256], P('section', None, 'seq'), may hold values from -20 to 20
- lengths: int32 [8, 2, 4], P('section'), may hold values from 1 to 1024, 2048 in all within a row
- order: int32 [8, 2], P('section'), may hold values from 0 to 1, each once within a row
Outputs:
- handoff: bfloat16 [8, 2, 2048, 4096], P('section', None, 'seq')
The draws below stay inside these ranges and needn't reach their ends.
Inputs may be any that keep to these rules, and one draw needn't show every extreme that they name: Each row holds the lengths of 4 documents packed end to end, summing to 2048, the longest exactly 1024. `order`: each row is a permutation of the microbatch numbers.
All inputs are finite; a program needn't handle non-finite values.
Results may differ from the reference program's by a relative error of at most 0.0037.
Values may be sent and summed in bfloat16 or wider, within the bound.
No kernel may reach another device: no remote copies, remote signals or barrier semaphores. Data moves between devices by JAX's collectives and lax.ppermute only.
A program may use at most 64 MiB of HBM per device.

```python
import math
import jax
import jax.numpy as jnp
import numpy as np
from jax import lax

HD = 128
QH = 32
KVH = 8
MB = 2
DOCS = 4
TOKENS = 2048
DOC_MAX = 1024
SECTIONS = 8


def draw_common(key):
    streams = jax.random.split(jax.random.fold_in(key, 7), 3)
    query_shape = (SECTIONS, MB, TOKENS, QH, HD)
    pair_shape = (SECTIONS, MB, TOKENS, KVH, HD)
    query_part = jax.random.truncated_normal(streams[0], -4.0, 4.0, query_shape, jnp.float32)
    key_part = jax.random.truncated_normal(streams[1], -4.0, 4.0, pair_shape, jnp.float32)
    value_part = jax.random.truncated_normal(streams[2], -4.0, 4.0, pair_shape, jnp.float32)
    return (query_part.reshape(SECTIONS, MB, TOKENS, QH * HD), jnp.concatenate([key_part, value_part], axis=-1))


def draw_queries(key, part):
    return draw_common(key)[0].astype(jnp.bfloat16)


def draw_keys_values(key, part):
    return draw_common(key)[1].astype(jnp.bfloat16)


def profile(number_of, total, reach, slope):
    loads = [(1 << 20) // math.isqrt(grade ** slope) + 1 for grade in range(2, number_of + 1)]
    surplus, holding = total - reach - (number_of - 1), [1] * (number_of - 1)
    while surplus > 0:
        candidates = [i for i in range(number_of - 1) if holding[i] < reach]
        whole, remaining = sum([loads[i] for i in candidates]), surplus
        for i in candidates:
            more = min(reach - holding[i], max(1, remaining * loads[i] // whole), surplus)
            holding[i] = holding[i] + more
            surplus = surplus - more
    return np.array([reach] + holding)


def uneven_parts(key, count, total, bound, skew):
    if count == 2:
        one = jax.random.randint(key, (), max(1, total - bound), min(bound, total - 1) + 1)
        return jnp.stack([one, total - one])
    tallies = jnp.asarray(profile(count, total, bound, skew), jnp.int32)
    couples = (count - 1) // 2
    giver, receiver = tallies[1:1 + 2 * couples:2], tallies[2:2 + 2 * couples:2]
    margin = jnp.minimum(giver - 1, bound - receiver)
    shifted = jax.random.randint(jax.random.fold_in(key, 1), (couples,), 0, 1 << 20) % (margin + 1)
    tallies = tallies.at[1:1 + 2 * couples:2].set(giver - shifted).at[2:2 + 2 * couples:2].set(receiver + shifted)
    return tallies[jax.random.permutation(jax.random.fold_in(key, 2), count)]


def setup_inputs(seed: int = 0) -> dict:
    key_list = jax.random.split(jax.random.key(seed), 5)
    return {
        "queries": draw_queries(jax.random.fold_in(key_list[4], 71), 0),
        "keys_values": draw_keys_values(jax.random.fold_in(key_list[4], 71), 0),
        "lengths": jax.vmap(lambda own: uneven_parts(own, DOCS, TOKENS, DOC_MAX, 2))(jax.random.split(key_list[2], SECTIONS * MB)).reshape((SECTIONS, MB, DOCS)).astype(jnp.int32),
        "order": jax.vmap(lambda own: jax.random.permutation(own, MB))(jax.random.split(key_list[3], SECTIONS)).reshape((SECTIONS, MB)).astype(jnp.int32),
    }


def segment_ids(lengths_row, rows_all):
    ends = jnp.cumsum(lengths_row).astype(jnp.int32)
    position = jnp.arange(rows_all, dtype=jnp.int32)
    return jnp.sum((position[:, None] >= ends[None, :]).astype(jnp.int32), axis=1).astype(jnp.int32)


def attend_one(operands):
    query_rows, pair_rows, lengths_row = operands
    rows_all = query_rows.shape[0]
    segment = segment_ids(lengths_row, rows_all)
    position = jnp.arange(rows_all, dtype=jnp.int32)
    allowed = (segment[:, None] == segment[None, :]) & (position[None, :] <= position[:, None])
    share = QH // KVH
    head_queries = jnp.transpose(query_rows.reshape(rows_all, QH, HD).astype(jnp.float32), (1, 0, 2))
    pairs = pair_rows.astype(jnp.float32)
    head_keys = jnp.repeat(jnp.transpose(pairs[:, :, :HD], (1, 0, 2)), share, axis=0)
    head_values = jnp.repeat(jnp.transpose(pairs[:, :, HD:], (1, 0, 2)), share, axis=0)

    def one_head(inputs):
        query_head, key_head, value_head = inputs
        scores = jnp.dot(query_head, key_head.T, precision=lax.Precision.HIGHEST) * (HD ** -0.5)
        peaks = jnp.max(jnp.where(allowed, scores, -jnp.inf), axis=1, keepdims=True)
        weights = jnp.where(allowed, jnp.exp(scores - peaks), jnp.float32(0.0))
        totals = jnp.sum(weights, axis=1, keepdims=True)
        rounded = lax.optimization_barrier(weights.astype(jnp.bfloat16)).astype(jnp.float32)
        mixed = jnp.dot(rounded, value_head, precision=lax.Precision.HIGHEST) / totals
        return mixed.astype(jnp.bfloat16)

    contexts = lax.map(one_head, (head_queries, head_keys, head_values))
    return jnp.transpose(contexts, (1, 0, 2)).reshape(rows_all, QH * HD)


def reference(queries, keys_values, lengths, order):
    flat_queries = queries.reshape(SECTIONS * MB, TOKENS, QH * HD)
    flat_pairs = keys_values.reshape(SECTIONS * MB, TOKENS, KVH, 2 * HD)
    flat_lengths = lengths.reshape(SECTIONS * MB, DOCS)
    contexts = lax.map(attend_one, (flat_queries, flat_pairs, flat_lengths))
    contexts = contexts.reshape(SECTIONS, MB, TOKENS, QH * HD)
    picked = jnp.take_along_axis(contexts, order[:, :, None, None].astype(jnp.int32), axis=1)
    return jnp.roll(picked, 1, axis=0)
```

```python
import functools

import jax
import jax.numpy as jnp
from jax import lax
from jax.experimental import pallas as pl
from jax.experimental.pallas import tpu as pltpu
from jax.sharding import PartitionSpec as P

HD = 128
QH = 32
KVH = 8
MB = 2
SHARE = QH // KVH
BLOCK = 128
EXPONENT = 1.4426950408889634 * HD ** (-0.5)
WINDOWS = (2, 4, 6, 8, 9)


def pack_kernel(q_ref, kv_ref, o_ref):
    wide = SHARE * HD
    for g in range(KVH):
        o_ref[g, :, 0:wide] = q_ref[0, 0, :, g * wide : (g + 1) * wide]
        o_ref[g, :, wide : wide + 2 * HD] = kv_ref[0, 0, :, g, :]


def pack(queries, keys_values):
    rows = queries.shape[2]
    wide = SHARE * HD + 2 * HD
    return pl.pallas_call(
        pack_kernel,
        out_shape=jax.ShapeDtypeStruct((MB * KVH, rows, wide), jnp.bfloat16),
        grid=(MB,),
        in_specs=[
            pl.BlockSpec((1, 1, rows, QH * HD), lambda m: (0, m, 0, 0)),
            pl.BlockSpec((1, 1, rows, KVH, 2 * HD), lambda m: (0, m, 0, 0, 0)),
        ],
        out_specs=pl.BlockSpec((KVH, rows, wide), lambda m: (m, 0, 0)),
        name="pack",
    )(queries, keys_values)


def attend_kernel(len_ref, q_ref, kv_ref, o_ref, ve_ref):
    i = pl.program_id(0)
    m = lax.axis_index("seq") // KVH

    @pl.when(i == 0)
    def _():
        ve_ref[:, 0:HD] = kv_ref[:, HD : 2 * HD]
        ve_ref[:, HD : 2 * HD] = jnp.ones((ve_ref.shape[0], HD), jnp.bfloat16)

    end0 = len_ref[0, m, 0]
    end1 = end0 + len_ref[0, m, 1]
    end2 = end1 + len_ref[0, m, 2]

    def start_of(t):
        late = jnp.where(t < end1, end0, jnp.where(t < end2, end1, end2))
        return jnp.where(t < end0, 0, late)

    first = i * BLOCK
    need = i + 1 - start_of(first) // BLOCK
    token = first + lax.broadcasted_iota(jnp.int32, (BLOCK, HD), 0)
    begin = start_of(token)
    lane = lax.broadcasted_iota(jnp.int32, (BLOCK, HD), 1)
    pair = 2

    def window(n):
        low = pl.multiple_of(jnp.maximum(i + 1 - n, 0) * BLOCK, BLOCK)
        keys = kv_ref[pl.ds(low, n * BLOCK), 0:HD]
        values = ve_ref[pl.ds(low, n * BLOCK), :]
        for h0 in range(0, SHARE, pair):
            heads = range(h0, h0 + pair)
            q = jnp.concatenate([q_ref[:, h * HD : (h + 1) * HD] for h in heads], axis=0)
            scores = lax.dot_general(
                q, keys, (((1,), (1,)), ((), ())), preferred_element_type=jnp.float32
            )
            tiles = []
            for j in range(n):
                key = low + j * BLOCK + lane
                allowed = key >= begin
                if j >= n - 2:
                    allowed = allowed & (key <= token)
                allowed = jnp.concatenate([allowed] * pair, axis=0)
                tiles.append(jnp.where(allowed, scores[:, j * BLOCK : (j + 1) * BLOCK], -jnp.inf))
            top = functools.reduce(jnp.maximum, tiles)
            peak = jnp.max(top, axis=1, keepdims=True) * EXPONENT
            weights = [jnp.exp2(t * EXPONENT - peak).astype(jnp.bfloat16) for t in tiles]
            mixed = jnp.dot(
                jnp.concatenate(weights, axis=1), values, preferred_element_type=jnp.float32
            )
            out = (mixed[:, 0:HD] / mixed[:, HD : 2 * HD]).astype(jnp.bfloat16)
            for k, h in enumerate(heads):
                o_ref[:, h * HD : (h + 1) * HD] = out[k * BLOCK : (k + 1) * BLOCK, :]

    below = 0
    for n in WINDOWS:
        pl.when((need > below) & (need <= n))(functools.partial(window, n))
        below = n


def attend(packed, lengths):
    tokens = packed.shape[0]
    wide = SHARE * HD
    return pl.pallas_call(
        attend_kernel,
        out_shape=jax.ShapeDtypeStruct((tokens, wide), jnp.bfloat16),
        grid_spec=pltpu.PrefetchScalarGridSpec(
            num_scalar_prefetch=1,
            grid=(tokens // BLOCK,),
            in_specs=[
                pl.BlockSpec((BLOCK, wide), lambda i, n: (i, 0)),
                pl.BlockSpec(
                    (tokens, 2 * HD), lambda i, n: (0, 2), pipeline_mode=pl.Buffered(1)
                ),
            ],
            out_specs=pl.BlockSpec((BLOCK, wide), lambda i, n: (i, 0)),
            scratch_shapes=[pltpu.VMEM((tokens, 2 * HD), jnp.bfloat16)],
        ),
        name="attend",
    )(lengths, packed, packed)


def unpack_kernel(order_ref, r_ref, o_ref):
    wide = SHARE * HD
    for g in range(KVH):
        o_ref[0, 0, :, g * wide : (g + 1) * wide] = r_ref[g]


def unpack(blocks, order):
    rows = blocks.shape[1]
    wide = SHARE * HD
    return pl.pallas_call(
        unpack_kernel,
        out_shape=jax.ShapeDtypeStruct((1, MB, rows, QH * HD), jnp.bfloat16),
        grid_spec=pltpu.PrefetchScalarGridSpec(
            num_scalar_prefetch=1,
            grid=(MB,),
            in_specs=[pl.BlockSpec((KVH, rows, wide), lambda j, o: (o[0, j], 0, 0))],
            out_specs=pl.BlockSpec((1, 1, rows, QH * HD), lambda j, o: (0, j, 0, 0)),
        ),
        name="unpack",
    )(order, blocks)


def exchange(blocks):
    return lax.all_to_all(blocks, "seq", split_axis=0, concat_axis=0, tiled=True)


def local(queries, keys_values, lengths, order):
    n_seq = MB * KVH
    rows = queries.shape[2]
    packed = exchange(pack(queries, keys_values))
    context = attend(packed.reshape(n_seq * rows, -1), lengths)
    back = exchange(context.reshape(n_seq, rows, SHARE * HD))
    sections = lax.axis_size("section")
    route = [(i, (i + 1) % sections) for i in range(sections)]
    return lax.ppermute(unpack(back, order), "section", route)


def solution(mesh):
    placed = (
        P("section", None, "seq", None),
        P("section", None, "seq", None, None),
        P("section", None, None),
        P("section", None),
    )
    return jax.shard_map(
        local,
        mesh=mesh,
        in_specs=placed,
        out_specs=P("section", None, "seq", None),
        check_vma=False,
    )
```

```python
import functools

import jax
import jax.numpy as jnp
from jax import lax
from jax.experimental import pallas as pl
from jax.experimental.pallas import tpu as pltpu
from jax.sharding import PartitionSpec as P

HD = 128
QH = 32
KVH = 8
MB = 2
SHARE = QH // KVH
ROWS = 256
TILE = 128
NEAR = SHARE // 2
EXPONENT = 1.4426950408889634 * HD ** (-0.5)
WINDOWS = 5


def pack_kernel(order_ref, q_ref, kv_ref, o_ref):
    wide = SHARE * HD
    for g in range(KVH):
        o_ref[g, :, 0:wide] = q_ref[0, 0, :, g * wide : (g + 1) * wide]
        o_ref[g, :, wide : wide + 2 * HD] = kv_ref[0, 0, :, g, :]


def pack(queries, keys_values, order):
    rows = queries.shape[2]
    wide = SHARE * HD + 2 * HD
    return pl.pallas_call(
        pack_kernel,
        out_shape=jax.ShapeDtypeStruct((MB * KVH, rows, wide), jnp.bfloat16),
        grid_spec=pltpu.PrefetchScalarGridSpec(
            num_scalar_prefetch=1,
            grid=(MB,),
            in_specs=[
                pl.BlockSpec((1, 1, rows, QH * HD), lambda j, o: (0, o[0, j], 0, 0)),
                pl.BlockSpec((1, 1, rows, KVH, 2 * HD), lambda j, o: (0, o[0, j], 0, 0, 0)),
            ],
            out_specs=pl.BlockSpec((KVH, rows, wide), lambda j, o: (j, 0, 0)),
        ),
        name="pack",
    )(order, queries, keys_values)


def attend_kernel(len_ref, order_ref, q_ref, kv_ref, near_ref, far_ref, ve_ref, s_ref, m_ref):
    i = pl.program_id(0)
    m = order_ref[0, lax.axis_index("seq") // KVH]

    @pl.when(i == 0)
    def _():
        ve_ref[:, 0:HD] = kv_ref[:, HD : 2 * HD]
        ve_ref[:, HD : 2 * HD] = jnp.ones((ve_ref.shape[0], HD), jnp.bfloat16)

    end0 = len_ref[0, m, 0]
    end1 = end0 + len_ref[0, m, 1]
    end2 = end1 + len_ref[0, m, 2]

    def start_of(t):
        late = jnp.where(t < end1, end0, jnp.where(t < end2, end1, end2))
        return jnp.where(t < end0, 0, late)

    need = i + 1 - start_of(i * ROWS) // ROWS
    token = i * ROWS + lax.broadcasted_iota(jnp.int32, (ROWS, TILE), 0)
    begin = start_of(token)
    lane = lax.broadcasted_iota(jnp.int32, (ROWS, TILE), 1)
    pair = 2
    last = ROWS // TILE

    def window(n):
        low = pl.multiple_of((i + 1 - n) * ROWS, ROWS)
        tiles = n * ROWS // TILE

        def score(g):
            heads = range(g * pair, (g + 1) * pair)
            q = jnp.concatenate([q_ref[:, h * HD : (h + 1) * HD] for h in heads], axis=0)
            scores = lax.dot_general(
                q,
                kv_ref[pl.ds(low, n * ROWS), 0:HD],
                (((1,), (1,)), ((), ())),
                preferred_element_type=jnp.float32,
            )
            top = None
            for j in range(tiles):
                key = low + j * TILE + lane
                allowed = key >= begin
                if j >= tiles - last:
                    allowed = allowed & (key <= token)
                allowed = jnp.concatenate([allowed] * pair, axis=0)
                tile = jnp.where(allowed, scores[:, j * TILE : (j + 1) * TILE], -jnp.inf)
                s_ref[g, :, j * TILE : (j + 1) * TILE] = tile
                top = tile if top is None else jnp.maximum(top, tile)
            peak = jnp.max(top, axis=1, keepdims=True)
            m_ref[g] = jnp.broadcast_to(peak, (pair * ROWS, TILE))

        def mix(g, o_ref):
            peak = m_ref[g]
            weights = [
                jnp.exp2((s_ref[g, :, j * TILE : (j + 1) * TILE] - peak) * EXPONENT).astype(
                    jnp.bfloat16
                )
                for j in range(tiles)
            ]
            mixed = jnp.dot(
                jnp.concatenate(weights, axis=1),
                ve_ref[pl.ds(low, n * ROWS), :],
                preferred_element_type=jnp.float32,
            )
            out = (mixed[:, 0:HD] / mixed[:, HD : 2 * HD]).astype(jnp.bfloat16)
            for h in range(pair):
                o_ref[:, h * HD : (h + 1) * HD] = out[h * ROWS : (h + 1) * ROWS, :]

        score(0)
        score(1)
        mix(0, near_ref)
        mix(1, far_ref)

    for n in range(1, WINDOWS + 1):
        pl.when(need == n)(functools.partial(window, n))


def attend(packed, lengths, order):
    tokens = packed.shape[0]
    wide = SHARE * HD
    half = NEAR * HD
    return pl.pallas_call(
        attend_kernel,
        out_shape=[jax.ShapeDtypeStruct((tokens, half), jnp.bfloat16)] * 2,
        grid_spec=pltpu.PrefetchScalarGridSpec(
            num_scalar_prefetch=2,
            grid=(tokens // ROWS,),
            in_specs=[
                pl.BlockSpec((ROWS, wide), lambda i, n, o: (i, 0)),
                pl.BlockSpec(
                    (tokens, 2 * HD), lambda i, n, o: (0, 2), pipeline_mode=pl.Buffered(1)
                ),
            ],
            out_specs=[pl.BlockSpec((ROWS, half), lambda i, n, o: (i, 0))] * 2,
            scratch_shapes=[
                pltpu.VMEM((tokens, 2 * HD), jnp.bfloat16),
                pltpu.VMEM((2, NEAR * ROWS, WINDOWS * ROWS), jnp.float32),
                pltpu.VMEM((2, NEAR * ROWS, TILE), jnp.float32),
            ],
        ),
        name="attend",
    )(lengths, order, packed, packed)


def unpack_kernel(near_ref, far_ref, o_ref, sems):
    copies = []
    for k in range(MB * KVH):
        for p, ref in enumerate((near_ref, far_ref)):
            part = ref.shape[2]
            col = (k % KVH) * SHARE * HD + p * part
            copies.append(
                pltpu.make_async_copy(
                    ref.at[k], o_ref.at[0, k // KVH, :, pl.ds(col, part)], sems.at[p, k]
                )
            )
    for copy in copies:
        copy.start()
    for copy in copies:
        copy.wait()


def unpack(near, far):
    rows = near.shape[1]
    return pl.pallas_call(
        unpack_kernel,
        out_shape=jax.ShapeDtypeStruct((1, MB, rows, QH * HD), jnp.bfloat16),
        in_specs=[pl.BlockSpec(memory_space=pltpu.VMEM)] * 2,
        out_specs=pl.BlockSpec(memory_space=pl.ANY),
        scratch_shapes=[pltpu.SemaphoreType.DMA((2, MB * KVH))],
        compiler_params=pltpu.CompilerParams(vmem_limit_bytes=8 << 20),
        name="unpack",
    )(near, far)


def exchange(blocks):
    return lax.all_to_all(blocks, "seq", split_axis=0, concat_axis=0, tiled=True)


def handed_on(block):
    sections = lax.axis_size("section")
    return lax.ppermute(block, "section", [(i, (i + 1) % sections) for i in range(sections)])


def handed_on(block):
    sections = lax.axis_size("section")
    return lax.ppermute(block, "section", [(i, (i + 1) % sections) for i in range(sections)])


def local(queries, keys_values, lengths, order):
    n_seq = MB * KVH
    rows = queries.shape[2]
    packed = exchange(pack(queries, keys_values, order)).reshape(n_seq * rows, -1)
    near, far = attend(packed, lengths, order)
    far = handed_on(far)
    near = handed_on(exchange(near.reshape(n_seq, rows, -1)))
    far = exchange(far.reshape(n_seq, rows, -1))
    return unpack(near, far)


def solution(mesh):
    placed = (
        P("section", None, "seq", None),
        P("section", None, "seq", None, None),
        P("section", None, None),
        P("section", None),
    )
    return jax.shard_map(
        local,
        mesh=mesh,
        in_specs=placed,
        out_specs=P("section", None, "seq", None),
        check_vma=False,
    )
```

```python
import functools

import jax
import jax.numpy as jnp
from jax import lax
from jax.experimental import pallas as pl
from jax.experimental.pallas import tpu as pltpu
from jax.sharding import PartitionSpec as P

HD = 128
QH = 32
KVH = 8
MB = 2
SHARE = QH // KVH
ROWS = 256
TILE = 128
NEAR = SHARE // 2
EXPONENT = 1.4426950408889634 * HD ** (-0.5)
WINDOWS = 5
GROUP = 32


def pack_kernel(order_ref, q_ref, kv_ref, o_ref, q_buf, kv_buf, pair_buf, q_in, kv_in, q_out, kv_out):
    wide = SHARE * HD
    slots = range(MB)
    loads = []
    for j in slots:
        m = order_ref[0, j]
        kv_load = pltpu.make_async_copy(kv_ref.at[0, m], kv_buf.at[j], kv_in.at[j])
        q_loads = [
            pltpu.make_async_copy(
                q_ref.at[0, m, :, pl.ds(g * wide, wide)], q_buf.at[j, g], q_in.at[j, g]
            )
            for g in range(KVH)
        ]
        loads.append((kv_load, q_loads))
    for kv_load, q_loads in loads:
        kv_load.start()
        for load in q_loads:
            load.start()
    span = GROUP * KVH
    row = lax.broadcasted_iota(jnp.int32, (span, span), 0)
    col = lax.broadcasted_iota(jnp.int32, (span, span), 1)
    source = (row & (GROUP - 1)) * KVH + row // GROUP
    sort = jnp.where(source == col, 1.0, 0.0).astype(jnp.bfloat16)
    stores = []
    for j in slots:
        kv_load, q_loads = loads[j]
        kv_load.wait()
        for t in range(0, kv_buf.shape[1], GROUP):
            mixed = kv_buf[j, t : t + GROUP].reshape(span, 2 * HD)
            split = jnp.dot(sort, mixed, preferred_element_type=jnp.float32).astype(jnp.bfloat16)
            for g in range(KVH):
                pair_buf[j, g, t : t + GROUP, :] = split[g * GROUP : (g + 1) * GROUP]
        for g in range(KVH):
            store = pltpu.make_async_copy(
                pair_buf.at[j, g],
                o_ref.at[j * KVH + g, :, pl.ds(wide, 2 * HD)],
                kv_out.at[j, g],
            )
            store.start()
            stores.append(store)
        for g in range(KVH):
            q_loads[g].wait()
            store = pltpu.make_async_copy(
                q_buf.at[j, g], o_ref.at[j * KVH + g, :, pl.ds(0, wide)], q_out.at[j, g]
            )
            store.start()
            stores.append(store)
    for store in stores:
        store.wait()


def pack(queries, keys_values, order):
    rows = queries.shape[2]
    wide = SHARE * HD
    return pl.pallas_call(
        pack_kernel,
        out_shape=jax.ShapeDtypeStruct((MB * KVH, rows, wide + 2 * HD), jnp.bfloat16),
        in_specs=[
            pl.BlockSpec(memory_space=pltpu.SMEM),
            pl.BlockSpec(memory_space=pl.ANY),
            pl.BlockSpec(memory_space=pl.ANY),
        ],
        out_specs=pl.BlockSpec(memory_space=pl.ANY),
        scratch_shapes=[
            pltpu.VMEM((MB, KVH, rows, wide), jnp.bfloat16),
            pltpu.VMEM((MB, rows, KVH, 2 * HD), jnp.bfloat16),
            pltpu.VMEM((MB, KVH, rows, 2 * HD), jnp.bfloat16),
            pltpu.SemaphoreType.DMA((MB, KVH)),
            pltpu.SemaphoreType.DMA((MB,)),
            pltpu.SemaphoreType.DMA((MB, KVH)),
            pltpu.SemaphoreType.DMA((MB, KVH)),
        ],
        name="pack",
    )(order, queries, keys_values)


def attend_kernel(
    len_ref, order_ref, x_ref, near_ref, far_ref, ve_ref, s_ref, m_ref, o_ref, sems
):
    m = order_ref[0, lax.axis_index("seq") // KVH]
    wide = SHARE * HD
    tokens = x_ref.shape[0]
    steps = tokens // ROWS
    ve_ref[:, 0:HD] = x_ref[:, wide + HD : wide + 2 * HD]
    ve_ref[:, HD : 2 * HD] = jnp.ones((tokens, HD), jnp.bfloat16)

    end0 = len_ref[0, m, 0]
    end1 = end0 + len_ref[0, m, 1]
    end2 = end1 + len_ref[0, m, 2]

    def start_of(t):
        late = jnp.where(t < end1, end0, jnp.where(t < end2, end1, end2))
        return jnp.where(t < end0, 0, late)

    lane = lax.broadcasted_iota(jnp.int32, (ROWS, TILE), 1)
    pair = 2
    last = ROWS // TILE
    outs = (near_ref, far_ref)

    def copy_out(g, i):
        rows = pl.ds(pl.multiple_of(i * ROWS, ROWS), ROWS)
        return pltpu.make_async_copy(o_ref.at[g, i], outs[g].at[rows, :], sems.at[g, i])

    def block(i, carry):
        row0 = pl.multiple_of(i * ROWS, ROWS)
        need = i + 1 - start_of(row0) // ROWS
        token = row0 + lax.broadcasted_iota(jnp.int32, (ROWS, TILE), 0)
        begin = start_of(token)

        def window(n):
            low = pl.multiple_of((i + 1 - n) * ROWS, ROWS)
            tiles = n * ROWS // TILE

            def score(g):
                heads = range(g * pair, (g + 1) * pair)
                q = jnp.concatenate(
                    [x_ref[pl.ds(row0, ROWS), h * HD : (h + 1) * HD] for h in heads], axis=0
                )
                scores = lax.dot_general(
                    q,
                    x_ref[pl.ds(low, n * ROWS), wide : wide + HD],
                    (((1,), (1,)), ((), ())),
                    preferred_element_type=jnp.float32,
                )
                top = None
                for j in range(tiles):
                    key = low + j * TILE + lane
                    allowed = key >= begin
                    if j >= tiles - last:
                        allowed = allowed & (key <= token)
                    allowed = jnp.concatenate([allowed] * pair, axis=0)
                    tile = jnp.where(allowed, scores[:, j * TILE : (j + 1) * TILE], -jnp.inf)
                    s_ref[g, :, j * TILE : (j + 1) * TILE] = tile
                    top = tile if top is None else jnp.maximum(top, tile)
                peak = jnp.max(top, axis=1, keepdims=True)
                m_ref[g] = jnp.broadcast_to(peak, (pair * ROWS, TILE))

            def mix(g):
                peak = m_ref[g]
                weights = [
                    jnp.exp2(
                        (s_ref[g, :, j * TILE : (j + 1) * TILE] - peak) * EXPONENT
                    ).astype(jnp.bfloat16)
                    for j in range(tiles)
                ]
                mixed = jnp.dot(
                    jnp.concatenate(weights, axis=1),
                    ve_ref[pl.ds(low, n * ROWS), :],
                    preferred_element_type=jnp.float32,
                )
                out = (mixed[:, 0:HD] / mixed[:, HD : 2 * HD]).astype(jnp.bfloat16)
                for h in range(pair):
                    o_ref[g, i, :, h * HD : (h + 1) * HD] = out[h * ROWS : (h + 1) * ROWS, :]

            score(0)
            score(1)
            mix(0)
            mix(1)

        for n in range(1, WINDOWS + 1):
            pl.when(need == n)(functools.partial(window, n))
        for g in range(2):
            copy_out(g, i).start()
        return carry

    lax.fori_loop(0, steps, block, 0)
    for g in range(2):
        for i in range(steps):
            copy_out(g, i).wait()


def attend(packed, lengths, order):
    tokens = packed.shape[0]
    half = NEAR * HD
    steps = tokens // ROWS
    return pl.pallas_call(
        attend_kernel,
        out_shape=[jax.ShapeDtypeStruct((tokens, half), jnp.bfloat16)] * 2,
        in_specs=[
            pl.BlockSpec(memory_space=pltpu.SMEM),
            pl.BlockSpec(memory_space=pltpu.SMEM),
            pl.BlockSpec(memory_space=pltpu.VMEM),
        ],
        out_specs=[pl.BlockSpec(memory_space=pl.ANY)] * 2,
        scratch_shapes=[
            pltpu.VMEM((tokens, 2 * HD), jnp.bfloat16),
            pltpu.VMEM((2, NEAR * ROWS, WINDOWS * ROWS), jnp.float32),
            pltpu.VMEM((2, NEAR * ROWS, TILE), jnp.float32),
            pltpu.VMEM((2, steps, ROWS, half), jnp.bfloat16),
            pltpu.SemaphoreType.DMA((2, steps)),
        ],
        compiler_params=pltpu.CompilerParams(vmem_limit_bytes=32 << 20),
        name="attend",
    )(lengths, order, packed)


def unpack_kernel(near_ref, far_ref, o_ref, sems):
    copies = []
    for k in range(MB * KVH):
        for p, ref in enumerate((near_ref, far_ref)):
            part = ref.shape[2]
            col = (k % KVH) * SHARE * HD + p * part
            copies.append(
                pltpu.make_async_copy(
                    ref.at[k], o_ref.at[0, k // KVH, :, pl.ds(col, part)], sems.at[p, k]
                )
            )
    for copy in copies:
        copy.start()
    for copy in copies:
        copy.wait()


def unpack(near, far):
    rows = near.shape[1]
    return pl.pallas_call(
        unpack_kernel,
        out_shape=jax.ShapeDtypeStruct((1, MB, rows, QH * HD), jnp.bfloat16),
        in_specs=[pl.BlockSpec(memory_space=pltpu.VMEM)] * 2,
        out_specs=pl.BlockSpec(memory_space=pl.ANY),
        scratch_shapes=[pltpu.SemaphoreType.DMA((2, MB * KVH))],
        compiler_params=pltpu.CompilerParams(vmem_limit_bytes=8 << 20),
        name="unpack",
    )(near, far)


def exchange(blocks):
    return lax.all_to_all(blocks, "seq", split_axis=0, concat_axis=0, tiled=True)


def handed_on(block):
    sections = lax.axis_size("section")
    return lax.ppermute(block, "section", [(i, (i + 1) % sections) for i in range(sections)])


def handed_on(block):
    sections = lax.axis_size("section")
    return lax.ppermute(block, "section", [(i, (i + 1) % sections) for i in range(sections)])


def local(queries, keys_values, lengths, order):
    n_seq = MB * KVH
    rows = queries.shape[2]
    packed = exchange(pack(queries, keys_values, order)).reshape(n_seq * rows, -1)
    near, far = attend(packed, lengths, order)
    far = handed_on(far)
    near = handed_on(exchange(near.reshape(n_seq, rows, -1)))
    far = exchange(far.reshape(n_seq, rows, -1))
    return unpack(near, far)


def solution(mesh):
    placed = (
        P("section", None, "seq", None),
        P("section", None, "seq", None, None),
        P("section", None, None),
        P("section", None),
    )
    return jax.shard_map(
        local,
        mesh=mesh,
        in_specs=placed,
        out_specs=P("section", None, "seq", None),
        check_vma=False,
    )
```

```python
import functools

import jax
import jax.numpy as jnp
from jax import lax
from jax.experimental import pallas as pl
from jax.experimental.pallas import tpu as pltpu
from jax.sharding import PartitionSpec as P


HD = 128
QH = 32
KVH = 8
MB = 2
SHARE = QH // KVH
ROWS = 256
TILE = 128
NEAR = SHARE // 2
EXPONENT = 1.4426950408889634 * HD ** (-0.5)
WINDOWS = 5
GROUP = 32


def pack_kernel(order_ref, q_ref, kv_ref, o_ref, q_buf, kv_buf, pair_buf, q_in, kv_in, q_out, kv_out):
    wide = SHARE * HD
    slots = range(MB)
    loads = []
    for j in slots:
        m = order_ref[0, j]
        kv_load = pltpu.make_async_copy(kv_ref.at[0, m], kv_buf.at[j], kv_in.at[j])
        q_loads = [
            pltpu.make_async_copy(
                q_ref.at[0, m, :, pl.ds(g * wide, wide)], q_buf.at[j, g], q_in.at[j, g]
            )
            for g in range(KVH)
        ]
        loads.append((kv_load, q_loads))
    for kv_load, q_loads in loads:
        kv_load.start()
        for load in q_loads:
            load.start()
    span = GROUP * KVH
    row = lax.broadcasted_iota(jnp.int32, (span, span), 0)
    col = lax.broadcasted_iota(jnp.int32, (span, span), 1)
    source = (row & (GROUP - 1)) * KVH + row // GROUP
    sort = jnp.where(source == col, 1.0, 0.0).astype(jnp.bfloat16)
    stores = []
    for j in slots:
        kv_load, q_loads = loads[j]
        kv_load.wait()
        for t in range(0, kv_buf.shape[1], GROUP):
            mixed = kv_buf[j, t : t + GROUP].reshape(span, 2 * HD)
            split = jnp.dot(sort, mixed, preferred_element_type=jnp.float32).astype(jnp.bfloat16)
            for g in range(KVH):
                pair_buf[j, g, t : t + GROUP, :] = split[g * GROUP : (g + 1) * GROUP]
        for g in range(KVH):
            store = pltpu.make_async_copy(
                pair_buf.at[j, g],
                o_ref.at[j * KVH + g, :, pl.ds(wide, 2 * HD)],
                kv_out.at[j, g],
            )
            store.start()
            stores.append(store)
        for g in range(KVH):
            q_loads[g].wait()
            store = pltpu.make_async_copy(
                q_buf.at[j, g], o_ref.at[j * KVH + g, :, pl.ds(0, wide)], q_out.at[j, g]
            )
            store.start()
            stores.append(store)
    for store in stores:
        store.wait()


def pack(queries, keys_values, order):
    rows = queries.shape[2]
    wide = SHARE * HD
    return pl.pallas_call(
        pack_kernel,
        out_shape=jax.ShapeDtypeStruct((MB * KVH, rows, wide + 2 * HD), jnp.bfloat16),
        in_specs=[
            pl.BlockSpec(memory_space=pltpu.SMEM),
            pl.BlockSpec(memory_space=pl.ANY),
            pl.BlockSpec(memory_space=pl.ANY),
        ],
        out_specs=pl.BlockSpec(memory_space=pl.ANY),
        scratch_shapes=[
            pltpu.VMEM((MB, KVH, rows, wide), jnp.bfloat16),
            pltpu.VMEM((MB, rows, KVH, 2 * HD), jnp.bfloat16),
            pltpu.VMEM((MB, KVH, rows, 2 * HD), jnp.bfloat16),
            pltpu.SemaphoreType.DMA((MB, KVH)),
            pltpu.SemaphoreType.DMA((MB,)),
            pltpu.SemaphoreType.DMA((MB, KVH)),
            pltpu.SemaphoreType.DMA((MB, KVH)),
        ],
        name="pack",
    )(order, queries, keys_values)


def attend_kernel(
    len_ref, order_ref, x_ref, near_ref, far_ref, ve_ref, s_ref, m_ref, o_ref, sems
):
    m = order_ref[0, lax.axis_index("seq") // KVH]
    wide = SHARE * HD
    tokens = x_ref.shape[0]
    steps = tokens // ROWS
    ve_ref[:, 0:HD] = x_ref[:, wide + HD : wide + 2 * HD]
    ve_ref[:, HD : 2 * HD] = jnp.ones((tokens, HD), jnp.bfloat16)

    end0 = len_ref[0, m, 0]
    end1 = end0 + len_ref[0, m, 1]
    end2 = end1 + len_ref[0, m, 2]

    def start_of(t):
        late = jnp.where(t < end1, end0, jnp.where(t < end2, end1, end2))
        return jnp.where(t < end0, 0, late)

    row = lax.broadcasted_iota(jnp.int32, (TILE, TILE), 0)
    lane = lax.broadcasted_iota(jnp.int32, (TILE, TILE), 1)
    diagonal = lane <= row
    halves = ROWS // TILE
    outs = (near_ref, far_ref)

    def copy_out(h, i):
        rows = pl.ds(pl.multiple_of(i * ROWS, ROWS), ROWS)
        cols = pl.ds((h % NEAR) * HD, HD)
        return pltpu.make_async_copy(
            o_ref.at[h, i], outs[h // NEAR].at[rows, cols], sems.at[h, i]
        )

    def block(i, carry):
        row0 = pl.multiple_of(i * ROWS, ROWS)
        need = i + 1 - start_of(row0) // ROWS
        begins = [start_of(row0 + k * TILE + row) for k in range(halves)]

        def window(n):
            low = pl.multiple_of((i + 1 - n) * ROWS, ROWS)

            def tiles(k):
                return (n - 1) * halves + k + 1

            def score(h):
                scores = lax.dot_general(
                    x_ref[pl.ds(row0, ROWS), h * HD : (h + 1) * HD],
                    x_ref[pl.ds(low, n * ROWS), wide : wide + HD],
                    (((1,), (1,)), ((), ())),
                    preferred_element_type=jnp.float32,
                )
                for k in range(halves):
                    rows = slice(k * TILE, (k + 1) * TILE)
                    top = None
                    for j in range(tiles(k)):
                        allowed = low + j * TILE + lane >= begins[k]
                        if j == tiles(k) - 1:
                            allowed = allowed & diagonal
                        tile = jnp.where(
                            allowed, scores[rows, j * TILE : (j + 1) * TILE], -jnp.inf
                        )
                        s_ref[h % 2, rows, j * TILE : (j + 1) * TILE] = tile
                        top = tile if top is None else jnp.maximum(top, tile)
                    peak = jnp.max(top, axis=1, keepdims=True)
                    m_ref[h % 2, rows, :] = jnp.broadcast_to(peak, (TILE, TILE))

            def mix(h):
                strips = []
                for k in range(halves):
                    rows = slice(k * TILE, (k + 1) * TILE)
                    peak = m_ref[h % 2, rows, :]
                    strip = [
                        jnp.exp2(
                            (s_ref[h % 2, rows, j * TILE : (j + 1) * TILE] - peak) * EXPONENT
                        ).astype(jnp.bfloat16)
                        for j in range(tiles(k))
                    ]
                    strip += [jnp.zeros((TILE, TILE), jnp.bfloat16)] * (n * halves - tiles(k))
                    strips.append(jnp.concatenate(strip, axis=1))
                mixed = jnp.dot(
                    jnp.concatenate(strips, axis=0),
                    ve_ref[pl.ds(low, n * ROWS), :],
                    preferred_element_type=jnp.float32,
                )
                o_ref[h, i] = (mixed[:, 0:HD] / mixed[:, HD : 2 * HD]).astype(jnp.bfloat16)

            score(0)
            for h in range(SHARE - 1):
                mix(h)
                score(h + 1)
            mix(SHARE - 1)

        for n in range(1, WINDOWS + 1):
            pl.when(need == n)(functools.partial(window, n))
        for h in range(SHARE):
            copy_out(h, i).start()
        return carry

    lax.fori_loop(0, steps, block, 0)
    for h in range(SHARE):
        for i in range(steps):
            copy_out(h, i).wait()


def attend(packed, lengths, order):
    tokens = packed.shape[0]
    half = NEAR * HD
    steps = tokens // ROWS
    return pl.pallas_call(
        attend_kernel,
        out_shape=[jax.ShapeDtypeStruct((tokens, half), jnp.bfloat16)] * 2,
        in_specs=[
            pl.BlockSpec(memory_space=pltpu.SMEM),
            pl.BlockSpec(memory_space=pltpu.SMEM),
            pl.BlockSpec(memory_space=pltpu.VMEM),
        ],
        out_specs=[pl.BlockSpec(memory_space=pl.ANY)] * 2,
        scratch_shapes=[
            pltpu.VMEM((tokens, 2 * HD), jnp.bfloat16),
            pltpu.VMEM((2, ROWS, WINDOWS * ROWS), jnp.float32),
            pltpu.VMEM((2, ROWS, TILE), jnp.float32),
            pltpu.VMEM((SHARE, steps, ROWS, HD), jnp.bfloat16),
            pltpu.SemaphoreType.DMA((SHARE, steps)),
        ],
        compiler_params=pltpu.CompilerParams(vmem_limit_bytes=32 << 20),
        name="attend",
    )(lengths, order, packed)


def unpack_kernel(near_ref, far_ref, o_ref, sems):
    copies = []
    for k in range(MB * KVH):
        for p, ref in enumerate((near_ref, far_ref)):
            part = ref.shape[2]
            col = (k % KVH) * SHARE * HD + p * part
            copies.append(
                pltpu.make_async_copy(
                    ref.at[k], o_ref.at[0, k // KVH, :, pl.ds(col, part)], sems.at[p, k]
                )
            )
    for copy in copies:
        copy.start()
    for copy in copies:
        copy.wait()


def unpack(near, far):
    rows = near.shape[1]
    return pl.pallas_call(
        unpack_kernel,
        out_shape=jax.ShapeDtypeStruct((1, MB, rows, QH * HD), jnp.bfloat16),
        in_specs=[pl.BlockSpec(memory_space=pltpu.VMEM)] * 2,
        out_specs=pl.BlockSpec(memory_space=pl.ANY),
        scratch_shapes=[pltpu.SemaphoreType.DMA((2, MB * KVH))],
        compiler_params=pltpu.CompilerParams(vmem_limit_bytes=8 << 20),
        name="unpack",
    )(near, far)


def exchange(blocks):
    return lax.all_to_all(blocks, "seq", split_axis=0, concat_axis=0, tiled=True)


def handed_on(block):
    sections = lax.axis_size("section")
    return lax.ppermute(block, "section", [(i, (i + 1) % sections) for i in range(sections)])


def handed_on(block):
    sections = lax.axis_size("section")
    return lax.ppermute(block, "section", [(i, (i + 1) % sections) for i in range(sections)])


def local(queries, keys_values, lengths, order):
    n_seq = MB * KVH
    rows = queries.shape[2]
    packed = exchange(pack(queries, keys_values, order)).reshape(n_seq * rows, -1)
    near, far = attend(packed, lengths, order)
    far = handed_on(far)
    near = exchange(near.reshape(n_seq, rows, -1))
    near = handed_on(near)
    far = exchange(far.reshape(n_seq, rows, -1))
    return unpack(near, far)


def solution(mesh):
    placed = (
        P("section", None, "seq", None),
        P("section", None, "seq", None, None),
        P("section", None, None),
        P("section", None),
    )
    return jax.shard_map(
        local,
        mesh=mesh,
        in_specs=placed,
        out_specs=P("section", None, "seq", None),
        check_vma=False,
    )
```

```python
import functools

import jax
import jax.numpy as jnp
from jax import lax
from jax.experimental import pallas as pl
from jax.experimental.pallas import tpu as pltpu
from jax.sharding import PartitionSpec as P


HD = 128
QH = 32
KVH = 8
MB = 2
SHARE = QH // KVH
ROWS = 256
TILE = 128
NEAR = SHARE // 2
EXPONENT = 1.4426950408889634 * HD ** (-0.5)
WINDOWS = 5
GROUP = 32


def pack_kernel(order_ref, q_ref, kv_ref, o_ref, kv_buf, q_in, kv_in):
    wide = SHARE * HD
    slots = range(MB)
    kv_loads, q_loads = [], []
    for j in slots:
        m = order_ref[0, j]
        kv_loads.append(pltpu.make_async_copy(kv_ref.at[0, m], kv_buf.at[j], kv_in.at[j]))
        q_loads += [
            pltpu.make_async_copy(
                q_ref.at[0, m, :, pl.ds(g * wide, wide)],
                o_ref.at[j * KVH + g, :, pl.ds(0, wide)],
                q_in.at[j, g],
            )
            for g in range(KVH)
        ]
    for load in kv_loads + q_loads:
        load.start()
    span = GROUP * KVH
    row = lax.broadcasted_iota(jnp.int32, (span, span), 0)
    col = lax.broadcasted_iota(jnp.int32, (span, span), 1)
    source = (row & (GROUP - 1)) * KVH + row // GROUP
    sort = jnp.where(source == col, 1.0, 0.0).astype(jnp.bfloat16)
    for j in slots:
        kv_loads[j].wait()
        for t in range(0, kv_buf.shape[1], GROUP):
            mixed = kv_buf[j, t : t + GROUP].reshape(span, 2 * HD)
            split = jnp.dot(sort, mixed, preferred_element_type=jnp.float32).astype(jnp.bfloat16)
            for g in range(KVH):
                o_ref[j * KVH + g, t : t + GROUP, wide : wide + 2 * HD] = split[
                    g * GROUP : (g + 1) * GROUP
                ]
    for load in q_loads:
        load.wait()


def pack(queries, keys_values, order):
    rows = queries.shape[2]
    wide = SHARE * HD
    return pl.pallas_call(
        pack_kernel,
        out_shape=jax.ShapeDtypeStruct((MB * KVH, rows, wide + 2 * HD), jnp.bfloat16),
        in_specs=[
            pl.BlockSpec(memory_space=pltpu.SMEM),
            pl.BlockSpec(memory_space=pltpu.HBM),
            pl.BlockSpec(memory_space=pltpu.HBM),
        ],
        out_specs=pl.BlockSpec(memory_space=pltpu.VMEM),
        scratch_shapes=[
            pltpu.VMEM((MB, rows, KVH, 2 * HD), jnp.bfloat16),
            pltpu.SemaphoreType.DMA((MB, KVH)),
            pltpu.SemaphoreType.DMA((MB,)),
        ],
        compiler_params=pltpu.CompilerParams(vmem_limit_bytes=12 << 20),
        name="pack",
    )(
        order,
        pltpu.with_memory_space_constraint(queries, pltpu.HBM),
        pltpu.with_memory_space_constraint(keys_values, pltpu.HBM),
    )


def attend_kernel(
    len_ref, order_ref, x_ref, near_ref, far_ref, ve_ref, s_ref, m_ref, o_ref, sems
):
    m = order_ref[0, lax.axis_index("seq") // KVH]
    wide = SHARE * HD
    tokens = x_ref.shape[0]
    steps = tokens // ROWS
    ve_ref[:, 0:HD] = x_ref[:, wide + HD : wide + 2 * HD]
    ve_ref[:, HD : 2 * HD] = jnp.ones((tokens, HD), jnp.bfloat16)

    end0 = len_ref[0, m, 0]
    end1 = end0 + len_ref[0, m, 1]
    end2 = end1 + len_ref[0, m, 2]

    def start_of(t):
        late = jnp.where(t < end1, end0, jnp.where(t < end2, end1, end2))
        return jnp.where(t < end0, 0, late)

    lane = lax.broadcasted_iota(jnp.int32, (ROWS, TILE), 1)
    pair = 2
    last = ROWS // TILE
    outs = (near_ref, far_ref)

    def copy_out(g, i):
        rows = pl.ds(pl.multiple_of(i * ROWS, ROWS), ROWS)
        return pltpu.make_async_copy(o_ref.at[g, i], outs[g].at[rows, :], sems.at[g, i])

    def block(i, carry):
        row0 = pl.multiple_of(i * ROWS, ROWS)
        need = i + 1 - start_of(row0) // ROWS
        token = row0 + lax.broadcasted_iota(jnp.int32, (ROWS, TILE), 0)
        begin = start_of(token)

        def window(n):
            low = pl.multiple_of((i + 1 - n) * ROWS, ROWS)
            tiles = n * ROWS // TILE

            def score(g):
                heads = range(g * pair, (g + 1) * pair)
                q = jnp.concatenate(
                    [x_ref[pl.ds(row0, ROWS), h * HD : (h + 1) * HD] for h in heads], axis=0
                )
                scores = lax.dot_general(
                    q,
                    x_ref[pl.ds(low, n * ROWS), wide : wide + HD],
                    (((1,), (1,)), ((), ())),
                    preferred_element_type=jnp.float32,
                )
                top = None
                for j in range(tiles):
                    key = low + j * TILE + lane
                    allowed = key >= begin
                    if j >= tiles - last:
                        allowed = allowed & (key <= token)
                    allowed = jnp.concatenate([allowed] * pair, axis=0)
                    tile = jnp.where(allowed, scores[:, j * TILE : (j + 1) * TILE], -jnp.inf)
                    s_ref[g, :, j * TILE : (j + 1) * TILE] = tile
                    top = tile if top is None else jnp.maximum(top, tile)
                peak = jnp.max(top, axis=1, keepdims=True)
                m_ref[g] = jnp.broadcast_to(peak, (pair * ROWS, TILE))

            def mix(g):
                peak = m_ref[g]
                weights = [
                    jnp.exp2(
                        (s_ref[g, :, j * TILE : (j + 1) * TILE] - peak) * EXPONENT
                    ).astype(jnp.bfloat16)
                    for j in range(tiles)
                ]
                mixed = jnp.dot(
                    jnp.concatenate(weights, axis=1),
                    ve_ref[pl.ds(low, n * ROWS), :],
                    preferred_element_type=jnp.float32,
                )
                out = (mixed[:, 0:HD] / mixed[:, HD : 2 * HD]).astype(jnp.bfloat16)
                for h in range(pair):
                    o_ref[g, i, :, h * HD : (h + 1) * HD] = out[h * ROWS : (h + 1) * ROWS, :]

            score(0)
            score(1)
            mix(0)
            mix(1)

        for n in range(1, WINDOWS + 1):
            pl.when(need == n)(functools.partial(window, n))
        for g in range(2):
            copy_out(g, i).start()
        return carry

    lax.fori_loop(0, steps, block, 0)
    for g in range(2):
        for i in range(steps):
            copy_out(g, i).wait()


def attend(packed, lengths, order):
    tokens = packed.shape[0]
    half = NEAR * HD
    steps = tokens // ROWS
    return pl.pallas_call(
        attend_kernel,
        out_shape=[jax.ShapeDtypeStruct((tokens, half), jnp.bfloat16)] * 2,
        in_specs=[
            pl.BlockSpec(memory_space=pltpu.SMEM),
            pl.BlockSpec(memory_space=pltpu.SMEM),
            pl.BlockSpec(memory_space=pltpu.VMEM),
        ],
        out_specs=[pl.BlockSpec(memory_space=pl.ANY)] * 2,
        scratch_shapes=[
            pltpu.VMEM((tokens, 2 * HD), jnp.bfloat16),
            pltpu.VMEM((2, NEAR * ROWS, WINDOWS * ROWS), jnp.float32),
            pltpu.VMEM((2, NEAR * ROWS, TILE), jnp.float32),
            pltpu.VMEM((2, steps, ROWS, half), jnp.bfloat16),
            pltpu.SemaphoreType.DMA((2, steps)),
        ],
        compiler_params=pltpu.CompilerParams(vmem_limit_bytes=32 << 20),
        name="attend",
    )(lengths, order, packed)


def unpack_kernel(near_ref, far_ref, o_ref, sems):
    copies = []
    for k in range(MB * KVH):
        for p, ref in enumerate((near_ref, far_ref)):
            part = ref.shape[2]
            col = (k % KVH) * SHARE * HD + p * part
            copies.append(
                pltpu.make_async_copy(
                    ref.at[k], o_ref.at[0, k // KVH, :, pl.ds(col, part)], sems.at[p, k]
                )
            )
    for copy in copies:
        copy.start()
    for copy in copies:
        copy.wait()


def unpack(near, far):
    rows = near.shape[1]
    return pl.pallas_call(
        unpack_kernel,
        out_shape=jax.ShapeDtypeStruct((1, MB, rows, QH * HD), jnp.bfloat16),
        in_specs=[pl.BlockSpec(memory_space=pltpu.VMEM)] * 2,
        out_specs=pl.BlockSpec(memory_space=pl.ANY),
        scratch_shapes=[pltpu.SemaphoreType.DMA((2, MB * KVH))],
        compiler_params=pltpu.CompilerParams(vmem_limit_bytes=8 << 20),
        name="unpack",
    )(near, far)


def exchange(blocks):
    return lax.all_to_all(blocks, "seq", split_axis=0, concat_axis=0, tiled=True)


def handed_on(block):
    sections = lax.axis_size("section")
    return lax.ppermute(block, "section", [(i, (i + 1) % sections) for i in range(sections)])


def handed_on(block):
    sections = lax.axis_size("section")
    return lax.ppermute(block, "section", [(i, (i + 1) % sections) for i in range(sections)])


def local(queries, keys_values, lengths, order):
    n_seq = MB * KVH
    rows = queries.shape[2]
    packed = exchange(pack(queries, keys_values, order)).reshape(n_seq * rows, -1)
    near, far = attend(packed, lengths, order)
    far = handed_on(far)
    near = exchange(near.reshape(n_seq, rows, -1))
    near = handed_on(near)
    far = exchange(far.reshape(n_seq, rows, -1))
    return unpack(near, far)


def solution(mesh):
    placed = (
        P("section", None, "seq", None),
        P("section", None, "seq", None, None),
        P("section", None, None),
        P("section", None),
    )
    return jax.shard_map(
        local,
        mesh=mesh,
        in_specs=placed,
        out_specs=P("section", None, "seq", None),
        check_vma=False,
    )
```

```python
import functools

import jax
import jax.numpy as jnp
from jax import lax
from jax.experimental import pallas as pl
from jax.experimental.pallas import tpu as pltpu
from jax.sharding import PartitionSpec as P


HD = 128
QH = 32
KVH = 8
MB = 2
SHARE = QH // KVH
ROWS = 256
TILE = 128
NEAR = SHARE // 2
EXPONENT = 1.4426950408889634 * HD ** (-0.5)
WINDOWS = 5
GROUP = 32


def pack_kernel(order_ref, q_ref, kv_ref, o_ref, kv_buf, q_in, kv_in):
    wide = SHARE * HD
    slots = range(MB)
    kv_loads, q_loads = [], []
    for j in slots:
        m = order_ref[0, j]
        kv_loads.append(pltpu.make_async_copy(kv_ref.at[0, m], kv_buf.at[j], kv_in.at[j]))
        q_loads += [
            pltpu.make_async_copy(
                q_ref.at[0, m, :, pl.ds(g * wide, wide)],
                o_ref.at[j * KVH + g, :, pl.ds(0, wide)],
                q_in.at[j, g],
            )
            for g in range(KVH)
        ]
    for load in kv_loads + q_loads:
        load.start()
    span = GROUP * KVH
    row = lax.broadcasted_iota(jnp.int32, (span, span), 0)
    col = lax.broadcasted_iota(jnp.int32, (span, span), 1)
    source = (row & (GROUP - 1)) * KVH + row // GROUP
    sort = jnp.where(source == col, 1.0, 0.0).astype(jnp.bfloat16)
    for j in slots:
        kv_loads[j].wait()
        for t in range(0, kv_buf.shape[1], GROUP):
            mixed = kv_buf[j, t : t + GROUP].reshape(span, 2 * HD)
            split = jnp.dot(sort, mixed, preferred_element_type=jnp.float32).astype(jnp.bfloat16)
            for g in range(KVH):
                o_ref[j * KVH + g, t : t + GROUP, wide : wide + 2 * HD] = split[
                    g * GROUP : (g + 1) * GROUP
                ]
    for load in q_loads:
        load.wait()


def pack(queries, keys_values, order):
    rows = queries.shape[2]
    wide = SHARE * HD
    return pl.pallas_call(
        pack_kernel,
        out_shape=jax.ShapeDtypeStruct((MB * KVH, rows, wide + 2 * HD), jnp.bfloat16),
        in_specs=[
            pl.BlockSpec(memory_space=pltpu.SMEM),
            pl.BlockSpec(memory_space=pltpu.HBM),
            pl.BlockSpec(memory_space=pltpu.HBM),
        ],
        out_specs=pl.BlockSpec(memory_space=pltpu.VMEM),
        scratch_shapes=[
            pltpu.VMEM((MB, rows, KVH, 2 * HD), jnp.bfloat16),
            pltpu.SemaphoreType.DMA((MB, KVH)),
            pltpu.SemaphoreType.DMA((MB,)),
        ],
        compiler_params=pltpu.CompilerParams(vmem_limit_bytes=12 << 20),
        name="pack",
    )(
        order,
        pltpu.with_memory_space_constraint(queries, pltpu.HBM),
        pltpu.with_memory_space_constraint(keys_values, pltpu.HBM),
    )


def attend_kernel(
    len_ref, order_ref, x_ref, near_ref, far_ref, ve_ref, s_ref, m_ref, o_ref, sems
):
    m = order_ref[0, lax.axis_index("seq") // KVH]
    wide = SHARE * HD
    tokens = x_ref.shape[0]
    steps = tokens // ROWS
    ve_ref[:, 0:HD] = x_ref[:, wide + HD : wide + 2 * HD]
    ve_ref[:, HD : 2 * HD] = jnp.ones((tokens, HD), jnp.bfloat16)

    end0 = len_ref[0, m, 0]
    end1 = end0 + len_ref[0, m, 1]
    end2 = end1 + len_ref[0, m, 2]

    def start_of(t):
        late = jnp.where(t < end1, end0, jnp.where(t < end2, end1, end2))
        return jnp.where(t < end0, 0, late)

    lane = lax.broadcasted_iota(jnp.int32, (ROWS, TILE), 1)
    pair = 2
    last = ROWS // TILE
    outs = (near_ref, far_ref)

    def copy_out(g, i):
        rows = pl.ds(pl.multiple_of(i * ROWS, ROWS), ROWS)
        return pltpu.make_async_copy(o_ref.at[g, i], outs[g].at[rows, :], sems.at[g, i])

    def block(i, carry):
        row0 = pl.multiple_of(i * ROWS, ROWS)
        need = i + 1 - start_of(row0) // ROWS
        token = row0 + lax.broadcasted_iota(jnp.int32, (ROWS, TILE), 0)
        begin = start_of(token)

        def window(n):
            low = pl.multiple_of((i + 1 - n) * ROWS, ROWS)
            tiles = n * ROWS // TILE

            def score(g):
                heads = range(g * pair, (g + 1) * pair)
                q = jnp.concatenate(
                    [x_ref[pl.ds(row0, ROWS), h * HD : (h + 1) * HD] for h in heads], axis=0
                )
                scores = lax.dot_general(
                    q,
                    x_ref[pl.ds(low, n * ROWS), wide : wide + HD],
                    (((1,), (1,)), ((), ())),
                    preferred_element_type=jnp.float32,
                )
                top = None
                for j in range(tiles):
                    key = low + j * TILE + lane
                    allowed = key >= begin
                    if j >= tiles - last:
                        allowed = allowed & (key <= token)
                    allowed = jnp.concatenate([allowed] * pair, axis=0)
                    tile = jnp.where(allowed, scores[:, j * TILE : (j + 1) * TILE], -jnp.inf)
                    s_ref[g, :, j * TILE : (j + 1) * TILE] = tile
                    top = tile if top is None else jnp.maximum(top, tile)
                peak = jnp.max(top, axis=1, keepdims=True)
                m_ref[g] = jnp.broadcast_to(peak, (pair * ROWS, TILE))

            def mix(g):
                peak = m_ref[g]

                def weigh(rows, j):
                    tile = s_ref[g, rows, j * TILE : (j + 1) * TILE]
                    return jnp.exp2((tile - peak[rows]) * EXPONENT).astype(jnp.bfloat16)

                weights = [weigh(slice(None), j) for j in range(tiles - 1)]
                ends = []
                for h in range(pair):
                    ends.append(jnp.zeros((TILE, TILE), jnp.bfloat16))
                    ends.append(weigh(slice(h * ROWS + TILE, (h + 1) * ROWS), tiles - 1))
                weights.append(jnp.concatenate(ends, axis=0))
                mixed = jnp.dot(
                    jnp.concatenate(weights, axis=1),
                    ve_ref[pl.ds(low, n * ROWS), :],
                    preferred_element_type=jnp.float32,
                )
                out = (mixed[:, 0:HD] / mixed[:, HD : 2 * HD]).astype(jnp.bfloat16)
                for h in range(pair):
                    o_ref[g, i, :, h * HD : (h + 1) * HD] = out[h * ROWS : (h + 1) * ROWS, :]

            score(0)
            score(1)
            mix(0)
            mix(1)

        for n in range(1, WINDOWS + 1):
            pl.when(need == n)(functools.partial(window, n))
        for g in range(2):
            copy_out(g, i).start()
        return carry

    lax.fori_loop(0, steps, block, 0)
    for g in range(2):
        for i in range(steps):
            copy_out(g, i).wait()


def attend(packed, lengths, order):
    tokens = packed.shape[0]
    half = NEAR * HD
    steps = tokens // ROWS
    return pl.pallas_call(
        attend_kernel,
        out_shape=[jax.ShapeDtypeStruct((tokens, half), jnp.bfloat16)] * 2,
        in_specs=[
            pl.BlockSpec(memory_space=pltpu.SMEM),
            pl.BlockSpec(memory_space=pltpu.SMEM),
            pl.BlockSpec(memory_space=pltpu.VMEM),
        ],
        out_specs=[pl.BlockSpec(memory_space=pl.ANY)] * 2,
        scratch_shapes=[
            pltpu.VMEM((tokens, 2 * HD), jnp.bfloat16),
            pltpu.VMEM((2, NEAR * ROWS, WINDOWS * ROWS), jnp.float32),
            pltpu.VMEM((2, NEAR * ROWS, TILE), jnp.float32),
            pltpu.VMEM((2, steps, ROWS, half), jnp.bfloat16),
            pltpu.SemaphoreType.DMA((2, steps)),
        ],
        compiler_params=pltpu.CompilerParams(vmem_limit_bytes=32 << 20),
        name="attend",
    )(lengths, order, packed)


def unpack_kernel(near_ref, far_ref, o_ref, sems):
    copies = []
    for k in range(MB * KVH):
        for p, ref in enumerate((near_ref, far_ref)):
            part = ref.shape[2]
            col = (k % KVH) * SHARE * HD + p * part
            copies.append(
                pltpu.make_async_copy(
                    ref.at[k], o_ref.at[0, k // KVH, :, pl.ds(col, part)], sems.at[p, k]
                )
            )
    for copy in copies:
        copy.start()
    for copy in copies:
        copy.wait()


def unpack(near, far):
    rows = near.shape[1]
    return pl.pallas_call(
        unpack_kernel,
        out_shape=jax.ShapeDtypeStruct((1, MB, rows, QH * HD), jnp.bfloat16),
        in_specs=[pl.BlockSpec(memory_space=pltpu.VMEM)] * 2,
        out_specs=pl.BlockSpec(memory_space=pl.ANY),
        scratch_shapes=[pltpu.SemaphoreType.DMA((2, MB * KVH))],
        compiler_params=pltpu.CompilerParams(vmem_limit_bytes=8 << 20),
        name="unpack",
    )(near, far)


def exchange(blocks):
    return lax.all_to_all(blocks, "seq", split_axis=0, concat_axis=0, tiled=True)


def handed_on(block):
    sections = lax.axis_size("section")
    return lax.ppermute(block, "section", [(i, (i + 1) % sections) for i in range(sections)])


def handed_on(block):
    sections = lax.axis_size("section")
    return lax.ppermute(block, "section", [(i, (i + 1) % sections) for i in range(sections)])


def local(queries, keys_values, lengths, order):
    n_seq = MB * KVH
    rows = queries.shape[2]
    packed = exchange(pack(queries, keys_values, order)).reshape(n_seq * rows, -1)
    near, far = attend(packed, lengths, order)
    far = handed_on(far)
    near = exchange(near.reshape(n_seq, rows, -1))
    near = handed_on(near)
    far = exchange(far.reshape(n_seq, rows, -1))
    return unpack(near, far)


def solution(mesh):
    placed = (
        P("section", None, "seq", None),
        P("section", None, "seq", None, None),
        P("section", None, None),
        P("section", None),
    )
    return jax.shard_map(
        local,
        mesh=mesh,
        in_specs=placed,
        out_specs=P("section", None, "seq", None),
        check_vma=False,
    )
```
